256 devices in a mesh: pipe: 32 (over y_hi, z, core), tensor: 8 (over y_lo, x).
Axes of the slice: x: 4, y: 4 (y_hi: 2, y_lo: 2; y = y_hi * 2 + y_lo), z: 8, core: 2. Of those that a mesh axis runs over, the one named last changes fastest.
Arguments:
- up_weight: bfloat16 [32, 6400, 3200], P('pipe', 'tensor'), may hold values from -0.109375 to 0.109375
- down_weight: bfloat16 [32, 6400, 3200], P('pipe', 'tensor'), may hold values from -0.078125 to 0.078125
- norm_gain: float32 [32, 3200], P('pipe'), may hold values from 0.1 to 1.9
- layer_scale: float32 [32, 3200], P('pipe'), may hold values from 0.25 to 1
- stash: bfloat16 [32, 3, 256, 3200], P('pipe', None, 'tensor'), may hold values from -6 to 6
- slot_order: int32 [32, 3], P('pipe'), may hold values from 0 to 2, each once within a row
- received: float32 [32, 256, 3200], P('pipe', 'tensor'), may hold values from -6 to 6
- arrivals: bfloat16 [3, 64, 12800], P(None, 'tensor'), may hold values from -6 to 6
Outputs:
- emitted: bfloat16 [32, 3, 256, 3200], P('pipe', None, 'tensor')
- pending: float32 [32, 256, 3200], P('pipe', 'tensor')
The draws below stay inside these ranges and needn't reach their ends.
Inputs may be any that keep to these rules, and one draw needn't show every extreme that they name: `slot_order`: each section's row is an ordering of the slots 0 to 2.
All inputs are finite; a program needn't handle non-finite values.
Results may differ from the reference program's by a relative error of at most 0.02.
Values may be sent and summed in bfloat16 or wider, within the bound.
No kernel may reach another device: no remote copies, remote signals or barrier semaphores. Data moves between devices by JAX's collectives and lax.ppermute only.
A program may use at most 128 MiB of HBM per device.

```python
import math
import jax
import jax.numpy as jnp
from jax import lax

D = 3200
HID = 6400
GRID = 16
TICKS = 3
TOK = 256
SECTIONS = 32
N_TENSOR = 8


def block_levels(stream_key, shape, split, least, largest):
    factor_of = 1.0
    for axis_at, parts in split:
        draws = jax.random.uniform(jax.random.fold_in(jax.random.fold_in(stream_key, 6), axis_at), (parts,), jnp.float32, least / len(split), largest / len(split))
        factor_of = factor_of * jnp.repeat(jnp.exp(draws), shape[axis_at] // parts).reshape((-1,) + (1,) * (len(shape) - 1 - axis_at))
    return factor_of


def centred(key, shape, width, most, split=(), held_as=jnp.bfloat16):
    level = block_levels(key, shape, split, -0.22, 0.18) if split else 1.0
    array = jax.random.normal(key, shape, jnp.float32) * width * level
    return jnp.minimum(jnp.maximum(array, -most), most).astype(held_as)


def setup_inputs(seed: int = 0) -> dict:
    key_of = jax.random.split(jax.random.key(seed), 9)
    return {
        "up_weight": centred(key_of[0], (SECTIONS, HID, D), D ** -0.5, 0.109375, ((0, 32), (1, 8))),
        "down_weight": centred(key_of[1], (SECTIONS, HID, D), HID ** -0.5, 0.078125, ((0, 32), (1, 8))),
        "norm_gain": jnp.clip(1.0 + 0.18 * jax.random.normal(key_of[2], (SECTIONS, D), jnp.float32), 0.1, 1.9),
        "layer_scale": jnp.clip(jnp.exp(math.log(1.0) - 1.3862944 * jax.random.uniform(key_of[3], (SECTIONS, D), jnp.float32) ** block_levels(key_of[3], (SECTIONS, D), ((0, 32),), -0.2, 0.2)), 0.25, 1.0),
        "stash": centred(key_of[4], (SECTIONS, TICKS, TOK, D), 1.0, 6.0, ((0, 32), (2, 8))),
        "slot_order": jax.vmap(lambda own: jax.random.permutation(own, TICKS))(jax.random.split(key_of[5], SECTIONS)).reshape((SECTIONS, TICKS)).astype(jnp.int32),
        "received": centred(key_of[6], (SECTIONS, TOK, D), 1.0, 6.0, ((0, 32), (1, 8)), jnp.float32),
        "arrivals": centred(key_of[7], (TICKS, TOK // 4, 4 * D), 1.0, 6.0, ((1, 8),)),
    }


EPS = 1e-06

def gelu_slope(hidden):
    return 0.5 * (1.0 + jax.scipy.special.erf(hidden * 0.7071067811865476)) + hidden * jnp.exp(-0.5 * hidden * hidden) * 0.3989422804014327

def norm_parts(stash_rows):
    values = stash_rows.astype(jnp.float32)
    factor = lax.rsqrt(lax.optimization_barrier(jnp.mean(values * values, axis=-1, keepdims=True)) + EPS)
    return (factor, values * factor)

def recompute(stash_rows, gain, up_w, down_w, scaled):
    factor, normed = norm_parts(stash_rows)
    act = (normed * gain).astype(jnp.bfloat16)
    dims = (((1,), (1,)), ((), ()))
    hidden = lax.dot_general(act, up_w, dims, preferred_element_type=jnp.float32)
    upstream = lax.dot_general(scaled, down_w, dims, preferred_element_type=jnp.float32)
    return (upstream * gelu_slope(hidden)).astype(jnp.bfloat16)

def norm_back(stash_rows, gain, total):
    factor, normed = norm_parts(stash_rows)
    scaled_back = total * gain
    return factor * (scaled_back - normed * lax.optimization_barrier(jnp.mean(scaled_back * normed, axis=-1, keepdims=True)))

def reference(up_weight, down_weight, norm_gain, layer_scale, stash, slot_order, received, arrivals):
    half = GRID // 2
    landed = arrivals.reshape(TICKS, half, half, 2, 2, D).transpose(0, 1, 3, 2, 4, 5).reshape(TICKS, TOK, D).astype(jnp.float32)
    block = HID // N_TENSOR

    def section(item):
        up_w, down_w, gain, lscale, stash_rows, grads = item
        scaled = (grads * lscale).astype(jnp.bfloat16)
        slope = recompute(stash_rows, gain, up_w, down_w, scaled)
        total = jnp.zeros((TOK, D), jnp.float32)
        for k in range(N_TENSOR):
            part = jnp.dot(slope[:, k * block:(k + 1) * block], up_w[k * block:(k + 1) * block], preferred_element_type=jnp.float32)
            part = lax.optimization_barrier(part.astype(jnp.bfloat16)).astype(jnp.float32)
            total = total + part
        return grads + norm_back(stash_rows, gain, total)
    grads = received
    emitted = []
    section_ids = jnp.arange(SECTIONS, dtype=jnp.int32)
    for tick in range(TICKS):
        chosen = stash[section_ids, slot_order[:, tick].astype(jnp.int32)]
        moved = lax.map(section, (up_weight, down_weight, norm_gain, layer_scale, chosen, grads))
        emitted.append(moved.astype(jnp.bfloat16))
        grads = jnp.concatenate([moved[1:], landed[tick][None]], axis=0)
    return (jnp.stack(emitted, axis=1), grads)
```

```python
import functools

import jax
import jax.numpy as jnp
from jax import lax
from jax.experimental import pallas as pl
from jax.experimental.pallas import tpu as pltpu
from jax.sharding import PartitionSpec as P

GRID = 16
EPS = 1e-06
LIMIT = 14 * 1024 * 1024
STEP = 1280
ROW = 4
NEAR = ((0, 0), (0, 1), (0, 3), (0, 2))
FAR = ((1, 0), (1, 1), (1, 3), (1, 2))
DIMS = (((1,), (1,)), ((), ()))
barrier = lax.optimization_barrier


def shifted(i, offset, sign):
    line, place = divmod(i, ROW)
    return (line + offset[0]) % 2 * ROW + (place + sign * offset[1]) % ROW


def to_peer(block, offset, sign):
    if offset == (0, 0):
        return block
    peers = lax.axis_size("tensor")
    return lax.ppermute(block, "tensor", [(i, shifted(i, offset, sign)) for i in range(peers)])


def to_peer_before(block, offset):
    peers, sections = lax.axis_size("tensor"), lax.axis_size("pipe")
    route = [
        (s * peers + i, (s - 1) % sections * peers + shifted(i, offset, 1))
        for s in range(sections)
        for i in range(peers)
    ]
    return lax.ppermute(block, ("pipe", "tensor"), route)


def to_section_before(block):
    sections = lax.axis_size("pipe")
    return lax.ppermute(block, "pipe", [(s, (s - 1) % sections) for s in range(sections)])


def from_section_before(block):
    sections = lax.axis_size("pipe")
    return lax.ppermute(block, "pipe", [(s, (s + 1) % sections) for s in range(sections)])


def owner_of(me, offset):
    line, place = lax.div(me, ROW), lax.rem(me, ROW)
    return lax.rem(line + offset[0], 2) * ROW + lax.rem(place + ROW - offset[1], ROW)


def gelu_slope(hidden):
    return (
        0.5 * (1.0 + lax.erf(hidden * 0.7071067811865476))
        + hidden * jnp.exp(-0.5 * hidden * hidden) * 0.3989422804014327
    )


def norm_parts(stash_rows):
    values = stash_rows.astype(jnp.float32)
    factor = lax.rsqrt(jnp.mean(values * values, axis=-1, keepdims=True) + EPS)
    return (factor, values * factor)


def bend_body(stash_ref, gain_ref, up_ref, out_ref):
    _, normed = norm_parts(stash_ref[...])
    act = (normed * gain_ref[...]).astype(jnp.bfloat16)
    hidden = lax.dot_general(act, up_ref[...], DIMS, preferred_element_type=jnp.float32)
    out_ref[...] = gelu_slope(hidden)


def bend_of(column, stashes, gain, up_w):
    tokens = stashes.shape[0]
    hidden, width = up_w.shape
    vmem = pl.BlockSpec(memory_space=pltpu.VMEM)
    return pl.pallas_call(
        bend_body,
        out_shape=jax.ShapeDtypeStruct((tokens, hidden), jnp.float32),
        grid=(1,),
        in_specs=[pl.BlockSpec((tokens, width), lambda i: (0, column)), vmem, vmem],
        out_specs=vmem,
        compiler_params=pltpu.CompilerParams(vmem_limit_bytes=LIMIT),
        cost_estimate=pl.CostEstimate(
            flops=2 * tokens * width * hidden,
            bytes_accessed=2 * width * (hidden + tokens),
            transcendentals=2 * tokens * hidden,
        ),
        name="bend",
    )(stashes, gain, up_w)


def post_body(count, tick, last, meta_ref, slot_ref, *refs):
    homes = refs[:count]
    stash_ref, grads_ref, gain_ref, scale_ref, landed_ref = refs[count : count + 5]
    total = homes[0][...].astype(jnp.float32)
    for k in range(1, count):
        total = total + homes[k][...].astype(jnp.float32)
    factor, normed = norm_parts(stash_ref[slot_ref[0, tick]])
    back = total * gain_ref[...]
    back = factor * (back - normed * jnp.mean(back * normed, axis=-1, keepdims=True))
    moved = grads_ref[...].astype(jnp.float32) + back
    sent = jnp.where(meta_ref[1] == 0, landed_ref[tick].astype(jnp.float32), moved)
    if last:
        earlier, (out_ref, sent_ref) = refs[count + 5 : -2], refs[-2:]
        for k in range(tick):
            out_ref[k] = earlier[k][...]
        out_ref[tick] = moved.astype(jnp.bfloat16)
        sent_ref[...] = sent.astype(jnp.bfloat16)
    else:
        out_ref, sent_ref, scaled_ref = refs[count + 5 :]
        out_ref[...] = moved.astype(jnp.bfloat16)
        sent_ref[...] = sent.astype(jnp.bfloat16)
        scaled_ref[...] = (sent * scale_ref[...]).astype(jnp.bfloat16)


def post(tick, meta, slots, homes, stash, grads, gain, scale, landed, earlier):
    ticks = stash.shape[0]
    last = tick + 1 == ticks
    block = jax.ShapeDtypeStruct(homes[0].shape, jnp.bfloat16)
    smem = pl.BlockSpec(memory_space=pltpu.SMEM)
    vmem = pl.BlockSpec(memory_space=pltpu.VMEM)
    outs = [jax.ShapeDtypeStruct(stash.shape, jnp.bfloat16), block] if last else [block] * 3
    more = earlier if last else []
    return pl.pallas_call(
        functools.partial(post_body, len(homes), tick, last),
        out_shape=outs,
        in_specs=[smem] * 2 + [vmem] * (len(homes) + 5 + len(more)),
        out_specs=[vmem] * len(outs),
        compiler_params=pltpu.CompilerParams(vmem_limit_bytes=LIMIT),
        cost_estimate=pl.CostEstimate(
            flops=30 * homes[0].size, bytes_accessed=30 * homes[0].size, transcendentals=0
        ),
        name="post",
    )(meta, slots, *homes, stash, grads, gain, scale, landed, *more)


def chain_body(offsets, meta_ref, scaled_ref, bend_ref, down_ref, up_ref, *refs):
    count = len(NEAR)
    outs = refs[:count]
    rows, width = outs[0].shape
    bent_ref = bend_ref
    if offsets:
        bent_ref = refs[count]
        for k, offset in enumerate(offsets):
            start = pl.multiple_of(owner_of(meta_ref[0], offset) * rows, rows)
            bent_ref[k * rows : (k + 1) * rows, :] = bend_ref[pl.ds(start, rows), :]
    upstream = lax.dot_general(scaled_ref[...], down_ref[...], DIMS, preferred_element_type=jnp.float32)
    slope = (upstream * bent_ref[...]).astype(jnp.bfloat16)
    for c in range(0, width, STEP):
        stop = min(c + STEP, width)
        part = jnp.dot(slope, up_ref[:, c:stop], preferred_element_type=jnp.float32)
        part = part.astype(jnp.bfloat16)
        for k in range(count):
            outs[k][:, c:stop] = part[k * rows : (k + 1) * rows]


def chain(meta, offsets, scaled, column, bend, down_w, up_w):
    count = len(NEAR)
    hidden, width = down_w.shape
    tokens = scaled.shape[0]
    rows = tokens // count
    vmem = pl.BlockSpec(memory_space=pltpu.VMEM)
    return pl.pallas_call(
        functools.partial(chain_body, offsets),
        out_shape=[jax.ShapeDtypeStruct((rows, width), jnp.bfloat16)] * count,
        grid=(1,),
        in_specs=[
            pl.BlockSpec(memory_space=pltpu.SMEM),
            pl.BlockSpec((tokens, width), lambda i: (0, column)),
            vmem,
            vmem,
            vmem,
        ],
        out_specs=[vmem] * count,
        scratch_shapes=[pltpu.VMEM((tokens, hidden), jnp.float32)] if offsets else [],
        compiler_params=pltpu.CompilerParams(vmem_limit_bytes=LIMIT),
        cost_estimate=pl.CostEstimate(
            flops=4 * tokens * width * hidden,
            bytes_accessed=4 * width * hidden + 4 * tokens * width,
            transcendentals=0,
        ),
        name="chain",
    )(meta, scaled, bend, down_w, up_w)


def stack_body(count, *refs):
    rows = refs[0].shape[0]
    for k in range(count):
        refs[count][k * rows : (k + 1) * rows, :] = refs[k][...]


def stacked(blocks):
    count = len(blocks)
    rows, width = blocks[0].shape
    vmem = pl.BlockSpec(memory_space=pltpu.VMEM)
    return pl.pallas_call(
        functools.partial(stack_body, count),
        out_shape=jax.ShapeDtypeStruct((count * rows, width), blocks[0].dtype),
        in_specs=[vmem] * count,
        out_specs=vmem,
        compiler_params=pltpu.CompilerParams(vmem_limit_bytes=LIMIT),
        cost_estimate=pl.CostEstimate(
            flops=0, bytes_accessed=4 * count * rows * width, transcendentals=0
        ),
        name="stack",
    )(*blocks)


def prep_body(meta_ref, slot_ref, stash_ref, grads_ref, scale_ref, both_ref, later_ref):
    ticks, _, width = stash_ref.shape
    both_ref[:, :width] = stash_ref[slot_ref[0, 0]]
    both_ref[:, width:] = (grads_ref[...] * scale_ref[...]).astype(jnp.bfloat16)
    for tick in range(1, ticks):
        later_ref[:, (tick - 1) * width : tick * width] = stash_ref[slot_ref[0, tick]]


def prep(meta, slot_order, stash, grads, scale):
    ticks, rows, width = stash.shape
    vmem = pl.BlockSpec(memory_space=pltpu.VMEM)
    return pl.pallas_call(
        prep_body,
        out_shape=[
            jax.ShapeDtypeStruct((rows, 2 * width), jnp.bfloat16),
            jax.ShapeDtypeStruct((rows, (ticks - 1) * width), jnp.bfloat16),
        ],
        in_specs=[pl.BlockSpec(memory_space=pltpu.SMEM)] * 2 + [vmem] * 3,
        out_specs=[vmem] * 2,
        compiler_params=pltpu.CompilerParams(vmem_limit_bytes=LIMIT),
        cost_estimate=pl.CostEstimate(
            flops=stash.size, bytes_accessed=6 * stash.size, transcendentals=0
        ),
        name="prep",
    )(meta, slot_order, stash, grads, scale)


def load_body(*refs):
    half = len(refs) // 3
    copies = [pltpu.make_async_copy(refs[k], refs[half + k], refs[2 * half + k]) for k in range(half)]
    for copy in copies:
        copy.start()
    for copy in copies:
        copy.wait()


def loaded(*arrays):
    return pl.pallas_call(
        load_body,
        out_shape=[jax.ShapeDtypeStruct(a.shape, a.dtype) for a in arrays],
        in_specs=[pl.BlockSpec(memory_space=pl.ANY)] * len(arrays),
        out_specs=[pl.BlockSpec(memory_space=pltpu.VMEM)] * len(arrays),
        scratch_shapes=[pltpu.SemaphoreType.DMA] * len(arrays),
        compiler_params=pltpu.CompilerParams(vmem_limit_bytes=LIMIT),
        cost_estimate=pl.CostEstimate(
            flops=0, bytes_accessed=sum(2 * a.size * a.dtype.itemsize for a in arrays), transcendentals=0
        ),
        name="load",
    )(*arrays)


def shards(up_weight, down_weight, norm_gain, layer_scale, stash, slot_order, received, arrivals):
    up_w = up_weight[0]
    down_w = down_weight[0]
    rows = received.shape[1]
    width = received.shape[2]
    ticks = stash.shape[1]
    half = GRID // 2
    lines = rows // 4 // half
    landed = (
        arrivals.reshape(ticks, lines, half, 2, 2, width)
        .transpose(0, 1, 3, 2, 4, 5)
        .reshape(ticks, rows, width)
    )
    meta = jnp.stack([lax.axis_index("tensor"), lax.axis_index("pipe")]).astype(jnp.int32)
    grads = received[0]
    both, later = prep(meta, slot_order, stash[0], grads, layer_scale)
    later = lax.all_gather(later, "tensor", axis=0, tiled=True)
    blocks = [to_peer(both, o, 1) for o in NEAR]
    up_w, down_w = loaded(up_w, down_w)
    scale_before = from_section_before(layer_scale)
    blocks[0], landed = barrier((blocks[0], landed))
    outputs = []
    for tick in range(ticks):
        near_scaled = stacked(blocks)
        far_scaled = to_peer(near_scaled, FAR[0], 1)
        if tick:
            offsets, bends, column = (NEAR, FAR), (bend, bend), 0
        else:
            bends = [bend_of(0, rows_of, norm_gain, up_w) for rows_of in (near_scaled, far_scaled)]
            offsets, column = (None, None), 1
        near = chain(meta, offsets[0], near_scaled, column, bends[0], down_w, up_w)
        home = [to_peer(p, o, -1) for p, o in zip(near, NEAR)]
        far = chain(meta, offsets[1], far_scaled, column, bends[1], down_w, up_w)
        home += [to_peer(p, o, -1) for p, o in zip(far, FAR)]
        if tick + 1 < ticks:
            later, _ = barrier((later, far[0]))
            bend = bend_of(tick, later, norm_gain, up_w)
            home[0], bend = barrier((home[0], bend))
        results = post(tick, meta, slot_order, home, stash[0], grads, norm_gain, scale_before, landed, outputs)
        outputs.append(results[0])
        if tick + 1 < ticks:
            blocks = [to_peer_before(results[2], o) for o in NEAR]
        grads = to_section_before(results[1])
    return (outputs[-1][None], grads.astype(jnp.float32)[None])


def solution(mesh):
    return jax.shard_map(
        shards,
        mesh=mesh,
        in_specs=(
            P("pipe", "tensor", None),
            P("pipe", "tensor", None),
            P("pipe", None),
            P("pipe", None),
            P("pipe", None, "tensor", None),
            P("pipe", None),
            P("pipe", "tensor", None),
            P(None, "tensor", None),
        ),
        out_specs=(P("pipe", None, "tensor", None), P("pipe", "tensor", None)),
        check_vma=False,
    )
```

```python
import functools

import jax
import jax.numpy as jnp
from jax import lax
from jax.experimental import pallas as pl
from jax.experimental.pallas import tpu as pltpu
from jax.sharding import PartitionSpec as P

GRID = 16
EPS = 1e-06
LIMIT = 14 * 1024 * 1024
STEP = 640
HALVES = 2
PIECE = 32
ROW = 4
NEAR = ((0, 0), (0, 1), (0, 3), (0, 2))
FAR = ((1, 0), (1, 1), (1, 3), (1, 2))
DIMS = (((1,), (1,)), ((), ()))
barrier = lax.optimization_barrier


def shifted(i, offset, sign):
    line, place = divmod(i, ROW)
    return (line + offset[0]) % 2 * ROW + (place + sign * offset[1]) % ROW


def to_peer(block, offset, sign):
    if offset == (0, 0):
        return block
    peers = lax.axis_size("tensor")
    return lax.ppermute(block, "tensor", [(i, shifted(i, offset, sign)) for i in range(peers)])


def to_section_before(block):
    sections = lax.axis_size("pipe")
    return lax.ppermute(block, "pipe", [(s, (s - 1) % sections) for s in range(sections)])


def gelu_slope(hidden):
    return (
        0.5 * (1.0 + lax.erf(hidden * 0.7071067811865476))
        + hidden * jnp.exp(-0.5 * hidden * hidden) * 0.3989422804014327
    )


def norm_parts(stash_rows):
    values = stash_rows.astype(jnp.float32)
    factor = lax.rsqrt(jnp.mean(values * values, axis=-1, keepdims=True) + EPS)
    return (factor, values * factor)


def bend_body(stash_ref, gain_ref, up_ref, out_ref, act_ref):
    halves, tokens, width = out_ref.shape

    def rows_at(i, carry):
        own = pl.ds(pl.multiple_of(i * PIECE, PIECE), PIECE)
        _, normed = norm_parts(stash_ref[own, :])
        act_ref[own, :] = (normed * gain_ref[...]).astype(jnp.bfloat16)
        return carry

    def half_at(h, carry):
        units = pl.ds(pl.multiple_of(h * width, 16), width)
        hidden = lax.dot_general(act_ref[...], up_ref[units, :], DIMS, preferred_element_type=jnp.float32)
        out_ref[h] = gelu_slope(hidden)
        return carry

    lax.fori_loop(0, tokens // PIECE, rows_at, 0)
    lax.fori_loop(0, halves, half_at, 0)


def bend_of(column, stashes, gain, up_w):
    tokens = stashes.shape[0]
    hidden, width = up_w.shape
    vmem = pl.BlockSpec(memory_space=pltpu.VMEM)
    return pl.pallas_call(
        bend_body,
        out_shape=jax.ShapeDtypeStruct((HALVES, tokens, hidden // HALVES), jnp.float32),
        grid=(1,),
        in_specs=[pl.BlockSpec((tokens, width), lambda i: (0, column)), vmem, vmem],
        out_specs=vmem,
        scratch_shapes=[pltpu.VMEM((tokens, width), jnp.bfloat16)],
        compiler_params=pltpu.CompilerParams(vmem_limit_bytes=LIMIT),
        cost_estimate=pl.CostEstimate(
            flops=2 * tokens * width * hidden,
            bytes_accessed=2 * width * (hidden + tokens),
            transcendentals=2 * tokens * hidden,
        ),
        name="bend",
    )(stashes, gain, up_w)


def post_body(count, tick, last, meta_ref, slot_ref, *refs):
    homes = refs[:count]
    stash_ref, grads_ref, gain_ref, landed_ref = refs[count : count + 4]
    total = homes[0][...].astype(jnp.float32)
    for k in range(1, count):
        total = total + homes[k][...].astype(jnp.float32)
    factor, normed = norm_parts(stash_ref[slot_ref[0, tick]])
    back = total * gain_ref[...]
    back = factor * (back - normed * jnp.mean(back * normed, axis=-1, keepdims=True))
    moved = grads_ref[...].astype(jnp.float32) + back
    sent = jnp.where(meta_ref[0] == 0, landed_ref[tick].astype(jnp.float32), moved)
    if last:
        earlier, (out_ref, sent_ref) = refs[count + 4 : -2], refs[-2:]
        for k in range(tick):
            out_ref[k] = earlier[k][...]
        out_ref[tick] = moved.astype(jnp.bfloat16)
        sent_ref[...] = sent.astype(jnp.bfloat16)
    else:
        out_ref, sent_ref = refs[count + 4 :]
        out_ref[...] = moved.astype(jnp.bfloat16)
        sent_ref[...] = sent.astype(jnp.bfloat16)


def post(tick, meta, slots, homes, stash, grads, gain, landed, earlier):
    ticks = stash.shape[0]
    last = tick + 1 == ticks
    block = jax.ShapeDtypeStruct(homes[0].shape, jnp.bfloat16)
    smem = pl.BlockSpec(memory_space=pltpu.SMEM)
    vmem = pl.BlockSpec(memory_space=pltpu.VMEM)
    outs = [jax.ShapeDtypeStruct(stash.shape, jnp.bfloat16), block] if last else [block] * 2
    more = earlier if last else []
    return pl.pallas_call(
        functools.partial(post_body, len(homes), tick, last),
        out_shape=outs,
        in_specs=[smem] * 2 + [vmem] * (len(homes) + 4 + len(more)),
        out_specs=[vmem] * len(outs),
        compiler_params=pltpu.CompilerParams(vmem_limit_bytes=LIMIT),
        cost_estimate=pl.CostEstimate(
            flops=30 * homes[0].size, bytes_accessed=30 * homes[0].size, transcendentals=0
        ),
        name="post",
    )(meta, slots, *homes, stash, grads, gain, landed, *more)


def chain_body(scaled_ref, bend_ref, down_ref, up_ref, *refs):
    count = len(NEAR)
    outs, slope_ref = refs[:count], refs[count]
    rows, width = outs[0].shape
    halves, _, units = bend_ref.shape

    def half_at(h, carry):
        own = pl.ds(pl.multiple_of(h * units, 16), units)
        upstream = lax.dot_general(scaled_ref[...], down_ref[own, :], DIMS, preferred_element_type=jnp.float32)
        slope_ref[h] = (upstream * bend_ref[h]).astype(jnp.bfloat16)
        return carry

    def columns_at(c, carry):
        own = pl.ds(pl.multiple_of(c * STEP, 128), STEP)
        part = sum(
            jnp.dot(slope_ref[h], up_ref[h * units : (h + 1) * units, own], preferred_element_type=jnp.float32)
            for h in range(halves)
        )
        part = part.astype(jnp.bfloat16)
        for k in range(count):
            outs[k][:, own] = part[k * rows : (k + 1) * rows]
        return carry

    lax.fori_loop(0, halves, half_at, 0)
    lax.fori_loop(0, width // STEP, columns_at, 0)


def chain(scaled, column, bend, down_w, up_w):
    count = len(NEAR)
    hidden, width = down_w.shape
    tokens = scaled.shape[0]
    rows = tokens // count
    vmem = pl.BlockSpec(memory_space=pltpu.VMEM)
    return pl.pallas_call(
        chain_body,
        out_shape=[jax.ShapeDtypeStruct((rows, width), jnp.bfloat16)] * count,
        grid=(1,),
        in_specs=[pl.BlockSpec((tokens, width), lambda i: (0, column)), vmem, vmem, vmem],
        out_specs=[vmem] * count,
        scratch_shapes=[pltpu.VMEM((HALVES, tokens, hidden // HALVES), jnp.bfloat16)],
        compiler_params=pltpu.CompilerParams(vmem_limit_bytes=LIMIT),
        cost_estimate=pl.CostEstimate(
            flops=4 * tokens * width * hidden,
            bytes_accessed=4 * width * hidden + 4 * tokens * width,
            transcendentals=0,
        ),
        name="chain",
    )(scaled, bend, down_w, up_w)


def rescale_body(grads_ref, scale_ref, out_ref):
    out_ref[...] = (grads_ref[...].astype(jnp.float32) * scale_ref[...]).astype(jnp.bfloat16)


def rescaled(grads, scale):
    vmem = pl.BlockSpec(memory_space=pltpu.VMEM)
    return pl.pallas_call(
        rescale_body,
        out_shape=jax.ShapeDtypeStruct(grads.shape, jnp.bfloat16),
        in_specs=[vmem] * 2,
        out_specs=vmem,
        compiler_params=pltpu.CompilerParams(vmem_limit_bytes=LIMIT),
        cost_estimate=pl.CostEstimate(
            flops=grads.size, bytes_accessed=4 * grads.size, transcendentals=0
        ),
        name="rescale",
    )(grads, scale)


def stack_body(count, *refs):
    rows = refs[0].shape[0]
    for k in range(count):
        refs[count][k * rows : (k + 1) * rows, :] = refs[k][...]


def stacked(blocks):
    count = len(blocks)
    rows, width = blocks[0].shape
    vmem = pl.BlockSpec(memory_space=pltpu.VMEM)
    return pl.pallas_call(
        functools.partial(stack_body, count),
        out_shape=jax.ShapeDtypeStruct((count * rows, width), blocks[0].dtype),
        in_specs=[vmem] * count,
        out_specs=vmem,
        compiler_params=pltpu.CompilerParams(vmem_limit_bytes=LIMIT),
        cost_estimate=pl.CostEstimate(
            flops=0, bytes_accessed=4 * count * rows * width, transcendentals=0
        ),
        name="stack",
    )(*blocks)


def prep_body(slot_ref, stash_ref, grads_ref, scale_ref, both_ref, *later_refs):
    width = stash_ref.shape[2]
    both_ref[:, :width] = stash_ref[slot_ref[0, 0]]
    both_ref[:, width:] = (grads_ref[...] * scale_ref[...]).astype(jnp.bfloat16)
    for k, later_ref in enumerate(later_refs):
        later_ref[...] = stash_ref[slot_ref[0, k + 1]]


def prep(slot_order, stash, grads, scale):
    ticks, rows, width = stash.shape
    vmem = pl.BlockSpec(memory_space=pltpu.VMEM)
    block = jax.ShapeDtypeStruct((rows, width), jnp.bfloat16)
    return pl.pallas_call(
        prep_body,
        out_shape=[jax.ShapeDtypeStruct((rows, 2 * width), jnp.bfloat16)] + [block] * (ticks - 1),
        in_specs=[pl.BlockSpec(memory_space=pltpu.SMEM)] + [vmem] * 3,
        out_specs=[vmem] * ticks,
        compiler_params=pltpu.CompilerParams(vmem_limit_bytes=LIMIT),
        cost_estimate=pl.CostEstimate(
            flops=stash.size, bytes_accessed=6 * stash.size, transcendentals=0
        ),
        name="prep",
    )(slot_order, stash, grads, scale)


def load_body(*refs):
    half = len(refs) // 3
    copies = [pltpu.make_async_copy(refs[k], refs[half + k], refs[2 * half + k]) for k in range(half)]
    for copy in copies:
        copy.start()
    for copy in copies:
        copy.wait()


def loaded(*arrays):
    return pl.pallas_call(
        load_body,
        out_shape=[jax.ShapeDtypeStruct(a.shape, a.dtype) for a in arrays],
        in_specs=[pl.BlockSpec(memory_space=pl.ANY)] * len(arrays),
        out_specs=[pl.BlockSpec(memory_space=pltpu.VMEM)] * len(arrays),
        scratch_shapes=[pltpu.SemaphoreType.DMA] * len(arrays),
        compiler_params=pltpu.CompilerParams(vmem_limit_bytes=LIMIT),
        cost_estimate=pl.CostEstimate(
            flops=0, bytes_accessed=sum(2 * a.size * a.dtype.itemsize for a in arrays), transcendentals=0
        ),
        name="load",
    )(*arrays)


def shards(up_weight, down_weight, norm_gain, layer_scale, stash, slot_order, received, arrivals):
    up_w = up_weight[0]
    down_w = down_weight[0]
    rows = received.shape[1]
    width = received.shape[2]
    ticks = stash.shape[1]
    half = GRID // 2
    lines = rows // 4 // half
    landed = (
        arrivals.reshape(ticks, lines, half, 2, 2, width)
        .transpose(0, 1, 3, 2, 4, 5)
        .reshape(ticks, rows, width)
    )
    meta = lax.axis_index("pipe").astype(jnp.int32).reshape(1)
    grads = received[0]
    both, *later = prep(slot_order, stash[0], grads, layer_scale)
    blocks = [to_peer(both, o, 1) for o in NEAR]
    up_w, down_w = loaded(up_w, down_w)
    blocks[0], landed = barrier((blocks[0], landed))
    near_scaled = stacked(blocks)
    far_scaled = to_peer(near_scaled, FAR[0], 1)
    near_bend = bend_of(0, near_scaled, norm_gain, up_w)
    far_bend = bend_of(0, far_scaled, norm_gain, up_w)
    outputs = []
    for tick in range(ticks):
        column = 0 if tick else 1
        if tick:
            near_scaled = stacked(blocks)
            far_scaled = to_peer(near_scaled, FAR[0], 1)
            far_bend = bend_of(0, far_stash, norm_gain, up_w)
        if tick + 1 < ticks:
            own_stash, _ = barrier((later[tick], near_scaled))
            near_stash = stacked([to_peer(own_stash, o, 1) for o in NEAR])
        near = chain(near_scaled, column, near_bend, down_w, up_w)
        home = [to_peer(p, o, -1) for p, o in zip(near, NEAR)]
        far = chain(far_scaled, column, far_bend, down_w, up_w)
        home += [to_peer(p, o, -1) for p, o in zip(far, FAR)]
        if tick + 1 < ticks:
            near_stash, _ = barrier((near_stash, far[0]))
            near_bend = bend_of(0, near_stash, norm_gain, up_w)
            home[0], near_bend = barrier((home[0], near_bend))
        results = post(tick, meta, slot_order, home, stash[0], grads, norm_gain, landed, outputs)
        outputs.append(results[0])
        grads = to_section_before(results[1])
        if tick + 1 < ticks:
            near_stash, _ = barrier((near_stash, results[1]))
            far_stash = to_peer(near_stash, FAR[0], 1)
            scaled = rescaled(grads, layer_scale)
            blocks = [to_peer(scaled, o, 1) for o in NEAR]
            blocks[0], far_stash = barrier((blocks[0], far_stash))
    return (outputs[-1][None], grads.astype(jnp.float32)[None])


def solution(mesh):
    return jax.shard_map(
        shards,
        mesh=mesh,
        in_specs=(
            P("pipe", "tensor", None),
            P("pipe", "tensor", None),
            P("pipe", None),
            P("pipe", None),
            P("pipe", None, "tensor", None),
            P("pipe", None),
            P("pipe", "tensor", None),
            P(None, "tensor", None),
        ),
        out_specs=(P("pipe", None, "tensor", None), P("pipe", "tensor", None)),
        check_vma=False,
    )
```

```python
import functools

import jax
import jax.numpy as jnp
from jax import lax
from jax.experimental import pallas as pl
from jax.experimental.pallas import tpu as pltpu
from jax.sharding import PartitionSpec as P

GRID = 16
EPS = 1e-06
LIMIT = 14 * 1024 * 1024
STEP = 640
HALVES = 2
PIECE = 32
BAND = 16
ROW = 4
NEAR = ((0, 0), (0, 1), (0, 3), (0, 2))
FAR = ((1, 0), (1, 1), (1, 3), (1, 2))
DIMS = (((1,), (1,)), ((), ()))
barrier = lax.optimization_barrier


def shifted(i, offset, sign):
    line, place = divmod(i, ROW)
    return (line + offset[0]) % 2 * ROW + (place + sign * offset[1]) % ROW


def to_peer(block, offset, sign):
    if offset == (0, 0):
        return block
    peers = lax.axis_size("tensor")
    return lax.ppermute(block, "tensor", [(i, shifted(i, offset, sign)) for i in range(peers)])


def to_section_before(block):
    sections = lax.axis_size("pipe")
    return lax.ppermute(block, "pipe", [(s, (s - 1) % sections) for s in range(sections)])


def gelu_slope(hidden):
    return (
        0.5 * (1.0 + lax.erf(hidden * 0.7071067811865476))
        + hidden * jnp.exp(-0.5 * hidden * hidden) * 0.3989422804014327
    )


def norm_parts(stash_rows):
    values = stash_rows.astype(jnp.float32)
    factor = lax.rsqrt(jnp.mean(values * values, axis=-1, keepdims=True) + EPS)
    return (factor, values * factor)


def bend_body(stash_ref, gain_ref, up_ref, out_ref, act_ref):
    halves, tokens, width = out_ref.shape

    def rows_at(i, carry):
        own = pl.ds(pl.multiple_of(i * PIECE, PIECE), PIECE)
        _, normed = norm_parts(stash_ref[own, :])
        act_ref[own, :] = (normed * gain_ref[...]).astype(jnp.bfloat16)
        return carry

    def half_at(h, carry):
        units = pl.ds(pl.multiple_of(h * width, 16), width)
        hidden = lax.dot_general(act_ref[...], up_ref[units, :], DIMS, preferred_element_type=jnp.float32)
        out_ref[h] = gelu_slope(hidden)
        return carry

    lax.fori_loop(0, tokens // PIECE, rows_at, 0)
    lax.fori_loop(0, halves, half_at, 0)


def bend_of(stashes, gain, up_w):
    tokens = stashes.shape[0]
    hidden, width = up_w.shape
    vmem = pl.BlockSpec(memory_space=pltpu.VMEM)
    return pl.pallas_call(
        bend_body,
        out_shape=jax.ShapeDtypeStruct((HALVES, tokens, hidden // HALVES), jnp.float32),
        in_specs=[vmem] * 3,
        out_specs=vmem,
        scratch_shapes=[pltpu.VMEM((tokens, width), jnp.bfloat16)],
        compiler_params=pltpu.CompilerParams(vmem_limit_bytes=LIMIT),
        cost_estimate=pl.CostEstimate(
            flops=2 * tokens * width * hidden,
            bytes_accessed=2 * width * (hidden + tokens),
            transcendentals=2 * tokens * hidden,
        ),
        name="bend",
    )(stashes, gain, up_w)


def post_body(count, tick, last, meta_ref, slot_ref, *refs):
    homes = refs[:count]
    stash_ref, grads_ref, gain_ref, landed_ref = refs[count : count + 4]
    earlier, (out_ref, sent_ref) = refs[count + 4 : -2], refs[-2:]

    def rows_at(i, carry):
        own = pl.ds(pl.multiple_of(i * BAND, BAND), BAND)
        total = homes[0][own, :].astype(jnp.float32)
        for k in range(1, count):
            total = total + homes[k][own, :].astype(jnp.float32)
        factor, normed = norm_parts(stash_ref[slot_ref[0, tick], own, :])
        back = total * gain_ref[...]
        back = factor * (back - normed * jnp.mean(back * normed, axis=-1, keepdims=True))
        moved = grads_ref[own, :].astype(jnp.float32) + back
        sent = jnp.where(meta_ref[0] == 0, landed_ref[tick, own, :].astype(jnp.float32), moved)
        sent_ref[own, :] = sent.astype(jnp.bfloat16)
        if last:
            for k in range(tick):
                out_ref[k, own, :] = earlier[k][own, :]
            out_ref[tick, own, :] = moved.astype(jnp.bfloat16)
        else:
            out_ref[own, :] = moved.astype(jnp.bfloat16)
        return carry

    lax.fori_loop(0, sent_ref.shape[0] // BAND, rows_at, 0)


def post(tick, meta, slots, homes, stash, grads, gain, landed, earlier):
    ticks = stash.shape[0]
    last = tick + 1 == ticks
    block = jax.ShapeDtypeStruct(homes[0].shape, jnp.bfloat16)
    smem = pl.BlockSpec(memory_space=pltpu.SMEM)
    vmem = pl.BlockSpec(memory_space=pltpu.VMEM)
    outs = [jax.ShapeDtypeStruct(stash.shape, jnp.bfloat16), block] if last else [block] * 2
    more = earlier if last else []
    return pl.pallas_call(
        functools.partial(post_body, len(homes), tick, last),
        out_shape=outs,
        in_specs=[smem] * 2 + [vmem] * (len(homes) + 4 + len(more)),
        out_specs=[vmem] * len(outs),
        compiler_params=pltpu.CompilerParams(vmem_limit_bytes=LIMIT),
        cost_estimate=pl.CostEstimate(
            flops=30 * homes[0].size, bytes_accessed=30 * homes[0].size, transcendentals=0
        ),
        name="post",
    )(meta, slots, *homes, stash, grads, gain, landed, *more)


def chain_body(scaled_ref, bend_ref, down_ref, up_ref, *refs):
    count = len(NEAR)
    outs, slope_ref = refs[:count], refs[count]
    rows, width = outs[0].shape
    halves, _, units = bend_ref.shape

    def half_at(h, carry):
        own = pl.ds(pl.multiple_of(h * units, 16), units)
        upstream = lax.dot_general(scaled_ref[...], down_ref[own, :], DIMS, preferred_element_type=jnp.float32)
        slope_ref[h] = (upstream * bend_ref[h]).astype(jnp.bfloat16)
        return carry

    def columns_at(c, carry):
        own = pl.ds(pl.multiple_of(c * STEP, 128), STEP)
        part = sum(
            jnp.dot(slope_ref[h], up_ref[h * units : (h + 1) * units, own], preferred_element_type=jnp.float32)
            for h in range(halves)
        )
        part = part.astype(jnp.bfloat16)
        for k in range(count):
            outs[k][:, own] = part[k * rows : (k + 1) * rows]
        return carry

    lax.fori_loop(0, halves, half_at, 0)
    lax.fori_loop(0, width // STEP, columns_at, 0)


def chain(scaled, bend, down_w, up_w):
    count = len(NEAR)
    hidden, width = down_w.shape
    tokens = scaled.shape[0]
    rows = tokens // count
    vmem = pl.BlockSpec(memory_space=pltpu.VMEM)
    return pl.pallas_call(
        chain_body,
        out_shape=[jax.ShapeDtypeStruct((rows, width), jnp.bfloat16)] * count,
        in_specs=[vmem] * 4,
        out_specs=[vmem] * count,
        scratch_shapes=[pltpu.VMEM((HALVES, tokens, hidden // HALVES), jnp.bfloat16)],
        compiler_params=pltpu.CompilerParams(vmem_limit_bytes=LIMIT),
        cost_estimate=pl.CostEstimate(
            flops=4 * tokens * width * hidden,
            bytes_accessed=4 * width * hidden + 4 * tokens * width,
            transcendentals=0,
        ),
        name="chain",
    )(scaled, bend, down_w, up_w)


def rescale_body(grads_ref, scale_ref, out_ref):
    out_ref[...] = (grads_ref[...].astype(jnp.float32) * scale_ref[...]).astype(jnp.bfloat16)


def rescaled(grads, scale):
    vmem = pl.BlockSpec(memory_space=pltpu.VMEM)
    return pl.pallas_call(
        rescale_body,
        out_shape=jax.ShapeDtypeStruct(grads.shape, jnp.bfloat16),
        in_specs=[vmem] * 2,
        out_specs=vmem,
        compiler_params=pltpu.CompilerParams(vmem_limit_bytes=LIMIT),
        cost_estimate=pl.CostEstimate(
            flops=grads.size, bytes_accessed=4 * grads.size, transcendentals=0
        ),
        name="rescale",
    )(grads, scale)


def stack_body(count, *refs):
    outs = refs[count:]
    rows = refs[0].shape[0]
    width = outs[0].shape[1]
    for c, out_ref in enumerate(outs):
        for k in range(count):
            out_ref[k * rows : (k + 1) * rows, :] = refs[k][:, c * width : (c + 1) * width]


def stacked(blocks, pieces=1):
    count = len(blocks)
    rows, width = blocks[0].shape
    vmem = pl.BlockSpec(memory_space=pltpu.VMEM)
    out = jax.ShapeDtypeStruct((count * rows, width // pieces), blocks[0].dtype)
    return pl.pallas_call(
        functools.partial(stack_body, count),
        out_shape=[out] * pieces,
        in_specs=[vmem] * count,
        out_specs=[vmem] * pieces,
        compiler_params=pltpu.CompilerParams(vmem_limit_bytes=LIMIT),
        cost_estimate=pl.CostEstimate(
            flops=0, bytes_accessed=4 * count * rows * width, transcendentals=0
        ),
        name="stack",
    )(*blocks)


def prep_body(slot_ref, stash_ref, grads_ref, scale_ref, now_ref, both_ref, later_ref):
    ticks, _, width = stash_ref.shape
    now_ref[...] = stash_ref[slot_ref[0, 0]]
    both_ref[:, :width] = now_ref[...]
    both_ref[:, width:] = (grads_ref[...] * scale_ref[...]).astype(jnp.bfloat16)
    for tick in range(1, ticks):
        later_ref[:, (tick - 1) * width : tick * width] = stash_ref[slot_ref[0, tick]]


def prep(slot_order, stash, grads, scale):
    ticks, rows, width = stash.shape
    vmem = pl.BlockSpec(memory_space=pltpu.VMEM)
    return pl.pallas_call(
        prep_body,
        out_shape=[jax.ShapeDtypeStruct((rows, k * width), jnp.bfloat16) for k in (1, 2, ticks - 1)],
        in_specs=[pl.BlockSpec(memory_space=pltpu.SMEM)] + [vmem] * 3,
        out_specs=[vmem] * 3,
        compiler_params=pltpu.CompilerParams(vmem_limit_bytes=LIMIT),
        cost_estimate=pl.CostEstimate(
            flops=stash.size, bytes_accessed=6 * stash.size, transcendentals=0
        ),
        name="prep",
    )(slot_order, stash, grads, scale)


def load_body(*refs):
    half = len(refs) // 3
    copies = [pltpu.make_async_copy(refs[k], refs[half + k], refs[2 * half + k]) for k in range(half)]
    for copy in copies:
        copy.start()
    for copy in copies:
        copy.wait()


def loaded(*arrays):
    return pl.pallas_call(
        load_body,
        out_shape=[jax.ShapeDtypeStruct(a.shape, a.dtype) for a in arrays],
        in_specs=[pl.BlockSpec(memory_space=pl.ANY)] * len(arrays),
        out_specs=[pl.BlockSpec(memory_space=pltpu.VMEM)] * len(arrays),
        scratch_shapes=[pltpu.SemaphoreType.DMA] * len(arrays),
        compiler_params=pltpu.CompilerParams(vmem_limit_bytes=LIMIT),
        cost_estimate=pl.CostEstimate(
            flops=0, bytes_accessed=sum(2 * a.size * a.dtype.itemsize for a in arrays), transcendentals=0
        ),
        name="load",
    )(*arrays)


def shards(up_weight, down_weight, norm_gain, layer_scale, stash, slot_order, received, arrivals):
    up_w = up_weight[0]
    down_w = down_weight[0]
    rows = received.shape[1]
    width = received.shape[2]
    ticks = stash.shape[1]
    half = GRID // 2
    lines = rows // 4 // half
    landed = (
        arrivals.reshape(ticks, lines, half, 2, 2, width)
        .transpose(0, 1, 3, 2, 4, 5)
        .reshape(ticks, rows, width)
    )
    meta = lax.axis_index("pipe").astype(jnp.int32).reshape(1)
    grads = received[0]
    now, both, later = prep(slot_order, stash[0], grads, layer_scale)
    blocks = [to_peer(both, o, 1) for o in NEAR]
    across = to_peer(now, FAR[0], 1)
    up_w, down_w = loaded(up_w, down_w)
    blocks[0], across, landed, up_w, down_w = barrier((blocks[0], across, landed, up_w, down_w))
    across = [to_peer(across, o, 1) for o in NEAR]
    near_stash, near_scaled = stacked(blocks, 2)
    far_scaled = to_peer(near_scaled, FAR[0], 1)
    near_bend = bend_of(near_stash, norm_gain, up_w)
    (far_stash,) = stacked(across)
    far_bend = bend_of(far_stash, norm_gain, up_w)
    later, _, _ = barrier((later, near_bend, far_stash))
    later_near = stacked([to_peer(later, o, 1) for o in NEAR], ticks - 1)
    outputs = []
    for tick in range(ticks):
        if tick:
            (near_scaled,) = stacked(blocks)
            far_scaled = to_peer(near_scaled, FAR[0], 1)
        near = chain(near_scaled, near_bend, down_w, up_w)
        home = [to_peer(p, o, -1) for p, o in zip(near, NEAR)]
        far = chain(far_scaled, far_bend, down_w, up_w)
        home += [to_peer(p, o, -1) for p, o in zip(far, FAR)]
        if tick + 1 < ticks:
            near_stash, _ = barrier((later_near[tick], far[0]))
            near_bend = bend_of(near_stash, norm_gain, up_w)
            home[0], near_bend = barrier((home[0], near_bend))
        results = post(tick, meta, slot_order, home, stash[0], grads, norm_gain, landed, outputs)
        outputs.append(results[0])
        grads = to_section_before(results[1])
        if tick + 1 < ticks:
            near_stash, _ = barrier((near_stash, results[1]))
            far_stash = to_peer(near_stash, FAR[0], 1)
            far_bend = bend_of(far_stash, norm_gain, up_w)
            scaled = rescaled(grads, layer_scale)
            blocks = [to_peer(scaled, o, 1) for o in NEAR]
            blocks[0], far_stash = barrier((blocks[0], far_stash))
    return (outputs[-1][None], grads.astype(jnp.float32)[None])


def solution(mesh):
    return jax.shard_map(
        shards,
        mesh=mesh,
        in_specs=(
            P("pipe", "tensor", None),
            P("pipe", "tensor", None),
            P("pipe", None),
            P("pipe", None),
            P("pipe", None, "tensor", None),
            P("pipe", None),
            P("pipe", "tensor", None),
            P(None, "tensor", None),
        ),
        out_specs=(P("pipe", None, "tensor", None), P("pipe", "tensor", None)),
        check_vma=False,
    )
```

```python
import functools

import jax
import jax.numpy as jnp
from jax import lax
from jax.experimental import pallas as pl
from jax.experimental.pallas import tpu as pltpu
from jax.sharding import PartitionSpec as P

GRID = 16
EPS = 1e-06
LIMIT = 14 * 1024 * 1024
WHOLE = 60 * 1024 * 1024
STEP = 640
HALVES = 2
PIECE = 32
BAND = 16
ROW = 4
NEAR = ((0, 0), (0, 1), (0, 3), (0, 2))
FAR = ((1, 0), (1, 1), (1, 3), (1, 2))
DIMS = (((1,), (1,)), ((), ()))
barrier = lax.optimization_barrier


def shifted(i, offset, sign):
    line, place = divmod(i, ROW)
    return (line + offset[0]) % 2 * ROW + (place + sign * offset[1]) % ROW


def to_peer(block, offset, sign):
    if offset == (0, 0):
        return block
    peers = lax.axis_size("tensor")
    return lax.ppermute(block, "tensor", [(i, shifted(i, offset, sign)) for i in range(peers)])


def to_section_before(block):
    sections = lax.axis_size("pipe")
    return lax.ppermute(block, "pipe", [(s, (s - 1) % sections) for s in range(sections)])


def gelu_slope(hidden):
    return (
        0.5 * (1.0 + lax.erf(hidden * 0.7071067811865476))
        + hidden * jnp.exp(-0.5 * hidden * hidden) * 0.3989422804014327
    )


def norm_parts(stash_rows):
    values = stash_rows.astype(jnp.float32)
    factor = lax.rsqrt(jnp.mean(values * values, axis=-1, keepdims=True) + EPS)
    return (factor, values * factor)


def bend_body(stash_ref, gain_ref, up_ref, out_ref, act_ref):
    halves, tokens, width = out_ref.shape

    def rows_at(i, carry):
        own = pl.ds(pl.multiple_of(i * PIECE, PIECE), PIECE)
        _, normed = norm_parts(stash_ref[own, :])
        act_ref[own, :] = (normed * gain_ref[...]).astype(jnp.bfloat16)
        return carry

    def half_at(h, carry):
        units = pl.ds(pl.multiple_of(h * width, 16), width)
        hidden = lax.dot_general(act_ref[...], up_ref[units, :], DIMS, preferred_element_type=jnp.float32)
        out_ref[h] = gelu_slope(hidden)
        return carry

    lax.fori_loop(0, tokens // PIECE, rows_at, 0)
    lax.fori_loop(0, halves, half_at, 0)


def bend_of(stashes, gain, up_w):
    tokens = stashes.shape[0]
    hidden, width = up_w.shape
    vmem = pl.BlockSpec(memory_space=pltpu.VMEM)
    return pl.pallas_call(
        bend_body,
        out_shape=jax.ShapeDtypeStruct((HALVES, tokens, hidden // HALVES), jnp.float32),
        in_specs=[vmem] * 3,
        out_specs=vmem,
        scratch_shapes=[pltpu.VMEM((tokens, width), jnp.bfloat16)],
        compiler_params=pltpu.CompilerParams(vmem_limit_bytes=LIMIT),
        cost_estimate=pl.CostEstimate(
            flops=2 * tokens * width * hidden,
            bytes_accessed=2 * width * (hidden + tokens),
            transcendentals=2 * tokens * hidden,
        ),
        name="bend",
    )(stashes, gain, up_w)


def post_body(count, tick, last, meta_ref, slot_ref, *refs):
    homes = refs[:count]
    stash_ref, grads_ref, gain_ref, landed_ref = refs[count : count + 4]
    earlier, (out_ref, sent_ref) = refs[count + 4 : -2], refs[-2:]

    def rows_at(i, carry):
        own = pl.ds(pl.multiple_of(i * BAND, BAND), BAND)
        total = homes[0][own, :].astype(jnp.float32)
        for k in range(1, count):
            total = total + homes[k][own, :].astype(jnp.float32)
        factor, normed = norm_parts(stash_ref[slot_ref[0, tick], own, :])
        back = total * gain_ref[...]
        back = factor * (back - normed * jnp.mean(back * normed, axis=-1, keepdims=True))
        moved = grads_ref[own, :].astype(jnp.float32) + back
        sent = jnp.where(meta_ref[0] == 0, landed_ref[tick, own, :].astype(jnp.float32), moved)
        sent_ref[own, :] = sent.astype(jnp.bfloat16)
        if last:
            for k in range(tick):
                out_ref[k, own, :] = earlier[k][own, :]
            out_ref[tick, own, :] = moved.astype(jnp.bfloat16)
        else:
            out_ref[own, :] = moved.astype(jnp.bfloat16)
        return carry

    lax.fori_loop(0, sent_ref.shape[0] // BAND, rows_at, 0)


def post(tick, meta, slots, homes, stash, grads, gain, landed, earlier):
    ticks = stash.shape[0]
    last = tick + 1 == ticks
    block = jax.ShapeDtypeStruct(homes[0].shape, jnp.bfloat16)
    smem = pl.BlockSpec(memory_space=pltpu.SMEM)
    vmem = pl.BlockSpec(memory_space=pltpu.VMEM)
    outs = [jax.ShapeDtypeStruct(stash.shape, jnp.bfloat16), block] if last else [block] * 2
    more = earlier if last else []
    return pl.pallas_call(
        functools.partial(post_body, len(homes), tick, last),
        out_shape=outs,
        in_specs=[smem] * 2 + [vmem] * (len(homes) + 4 + len(more)),
        out_specs=[vmem] * len(outs),
        compiler_params=pltpu.CompilerParams(vmem_limit_bytes=LIMIT),
        cost_estimate=pl.CostEstimate(
            flops=30 * homes[0].size, bytes_accessed=30 * homes[0].size, transcendentals=0
        ),
        name="post",
    )(meta, slots, *homes, stash, grads, gain, landed, *more)


def chain_body(scaled_ref, bend_ref, down_ref, up_ref, *refs):
    count = len(NEAR)
    outs, slope_ref = refs[:count], refs[count]
    rows, width = outs[0].shape
    halves, _, units = bend_ref.shape

    def half_at(h, carry):
        own = pl.ds(pl.multiple_of(h * units, 16), units)
        upstream = lax.dot_general(scaled_ref[...], down_ref[own, :], DIMS, preferred_element_type=jnp.float32)
        slope_ref[h] = (upstream * bend_ref[h]).astype(jnp.bfloat16)
        return carry

    def columns_at(c, carry):
        own = pl.ds(pl.multiple_of(c * STEP, 128), STEP)
        part = sum(
            jnp.dot(slope_ref[h], up_ref[h * units : (h + 1) * units, own], preferred_element_type=jnp.float32)
            for h in range(halves)
        )
        part = part.astype(jnp.bfloat16)
        for k in range(count):
            outs[k][:, own] = part[k * rows : (k + 1) * rows]
        return carry

    lax.fori_loop(0, halves, half_at, 0)
    lax.fori_loop(0, width // STEP, columns_at, 0)


def chain(scaled, bend, down_w, up_w):
    count = len(NEAR)
    hidden, width = down_w.shape
    tokens = scaled.shape[0]
    rows = tokens // count
    vmem = pl.BlockSpec(memory_space=pltpu.VMEM)
    return pl.pallas_call(
        chain_body,
        out_shape=[jax.ShapeDtypeStruct((rows, width), jnp.bfloat16)] * count,
        in_specs=[vmem] * 4,
        out_specs=[vmem] * count,
        scratch_shapes=[pltpu.VMEM((HALVES, tokens, hidden // HALVES), jnp.bfloat16)],
        compiler_params=pltpu.CompilerParams(vmem_limit_bytes=LIMIT),
        cost_estimate=pl.CostEstimate(
            flops=4 * tokens * width * hidden,
            bytes_accessed=4 * width * hidden + 4 * tokens * width,
            transcendentals=0,
        ),
        name="chain",
    )(scaled, bend, down_w, up_w)


def rescale_body(grads_ref, scale_ref, out_ref):
    out_ref[...] = (grads_ref[...].astype(jnp.float32) * scale_ref[...]).astype(jnp.bfloat16)


def rescaled(grads, scale):
    vmem = pl.BlockSpec(memory_space=pltpu.VMEM)
    return pl.pallas_call(
        rescale_body,
        out_shape=jax.ShapeDtypeStruct(grads.shape, jnp.bfloat16),
        in_specs=[vmem] * 2,
        out_specs=vmem,
        compiler_params=pltpu.CompilerParams(vmem_limit_bytes=LIMIT),
        cost_estimate=pl.CostEstimate(
            flops=grads.size, bytes_accessed=4 * grads.size, transcendentals=0
        ),
        name="rescale",
    )(grads, scale)


def stack_body(count, *refs):
    outs = refs[count:]
    rows = refs[0].shape[0]
    width = outs[0].shape[1]
    for c, out_ref in enumerate(outs):
        for k in range(count):
            out_ref[k * rows : (k + 1) * rows, :] = refs[k][:, c * width : (c + 1) * width]


def stacked(blocks, pieces=1):
    count = len(blocks)
    rows, width = blocks[0].shape
    vmem = pl.BlockSpec(memory_space=pltpu.VMEM)
    out = jax.ShapeDtypeStruct((count * rows, width // pieces), blocks[0].dtype)
    return pl.pallas_call(
        functools.partial(stack_body, count),
        out_shape=[out] * pieces,
        in_specs=[vmem] * count,
        out_specs=[vmem] * pieces,
        compiler_params=pltpu.CompilerParams(vmem_limit_bytes=LIMIT),
        cost_estimate=pl.CostEstimate(
            flops=0, bytes_accessed=4 * count * rows * width, transcendentals=0
        ),
        name="stack",
    )(*blocks)


def prep_body(slot_ref, stash_ref, grads_ref, scale_ref, now_ref, both_ref, later_ref):
    ticks, _, width = stash_ref.shape
    now_ref[...] = stash_ref[slot_ref[0, 0]]
    both_ref[:, :width] = now_ref[...]
    both_ref[:, width:] = (grads_ref[...] * scale_ref[...]).astype(jnp.bfloat16)
    for tick in range(1, ticks):
        later_ref[:, (tick - 1) * width : tick * width] = stash_ref[slot_ref[0, tick]]


def prep(slot_order, stash, grads, scale):
    ticks, rows, width = stash.shape
    vmem = pl.BlockSpec(memory_space=pltpu.VMEM)
    return pl.pallas_call(
        prep_body,
        out_shape=[jax.ShapeDtypeStruct((rows, k * width), jnp.bfloat16) for k in (1, 2, ticks - 1)],
        in_specs=[pl.BlockSpec(memory_space=pltpu.SMEM)] + [vmem] * 3,
        out_specs=[vmem] * 3,
        compiler_params=pltpu.CompilerParams(vmem_limit_bytes=WHOLE),
        cost_estimate=pl.CostEstimate(
            flops=stash.size, bytes_accessed=6 * stash.size, transcendentals=0
        ),
        name="prep",
    )(slot_order, stash, grads, scale)


def load_body(*refs):
    half = len(refs) // 3
    copies = [pltpu.make_async_copy(refs[k], refs[half + k], refs[2 * half + k]) for k in range(half)]
    for copy in copies:
        copy.start()
    for copy in copies:
        copy.wait()


def loaded(*arrays):
    return pl.pallas_call(
        load_body,
        out_shape=[jax.ShapeDtypeStruct(a.shape, a.dtype) for a in arrays],
        in_specs=[pl.BlockSpec(memory_space=pl.ANY)] * len(arrays),
        out_specs=[pl.BlockSpec(memory_space=pltpu.VMEM)] * len(arrays),
        scratch_shapes=[pltpu.SemaphoreType.DMA] * len(arrays),
        compiler_params=pltpu.CompilerParams(vmem_limit_bytes=LIMIT),
        cost_estimate=pl.CostEstimate(
            flops=0, bytes_accessed=sum(2 * a.size * a.dtype.itemsize for a in arrays), transcendentals=0
        ),
        name="load",
    )(*arrays)


def shards(up_weight, down_weight, norm_gain, layer_scale, stash, slot_order, received, arrivals):
    up_w = up_weight[0]
    down_w = down_weight[0]
    rows = received.shape[1]
    width = received.shape[2]
    ticks = stash.shape[1]
    half = GRID // 2
    lines = rows // 4 // half
    landed = (
        arrivals.reshape(ticks, lines, half, 2, 2, width)
        .transpose(0, 1, 3, 2, 4, 5)
        .reshape(ticks, rows, width)
    )
    meta = lax.axis_index("pipe").astype(jnp.int32).reshape(1)
    grads = received[0]
    now, both, later = prep(slot_order, stash[0], grads, layer_scale)
    blocks = [to_peer(both, o, 1) for o in NEAR]
    across = to_peer(now, FAR[0], 1)
    up_w, down_w = loaded(up_w, down_w)
    blocks[0], across, landed, up_w, down_w = barrier((blocks[0], across, landed, up_w, down_w))
    across = [to_peer(across, o, 1) for o in NEAR]
    near_stash, near_scaled = stacked(blocks, 2)
    far_scaled = to_peer(near_scaled, FAR[0], 1)
    near_bend = bend_of(near_stash, norm_gain, up_w)
    (far_stash,) = stacked(across)
    far_bend = bend_of(far_stash, norm_gain, up_w)
    later, _, _ = barrier((later, near_bend, far_stash))
    later_near = stacked([to_peer(later, o, 1) for o in NEAR], ticks - 1)
    outputs = []
    for tick in range(ticks):
        if tick:
            (near_scaled,) = stacked(blocks)
            far_scaled = to_peer(near_scaled, FAR[0], 1)
        near = chain(near_scaled, near_bend, down_w, up_w)
        home = [to_peer(p, o, -1) for p, o in zip(near, NEAR)]
        far = chain(far_scaled, far_bend, down_w, up_w)
        home += [to_peer(p, o, -1) for p, o in zip(far, FAR)]
        if tick + 1 < ticks:
            near_stash, _ = barrier((later_near[tick], far[0]))
            near_bend = bend_of(near_stash, norm_gain, up_w)
            home[0], near_bend = barrier((home[0], near_bend))
        results = post(tick, meta, slot_order, home, stash[0], grads, norm_gain, landed, outputs)
        outputs.append(results[0])
        grads = to_section_before(results[1])
        if tick + 1 < ticks:
            near_stash, _ = barrier((near_stash, results[1]))
            far_stash = to_peer(near_stash, FAR[0], 1)
            far_bend = bend_of(far_stash, norm_gain, up_w)
            scaled = rescaled(grads, layer_scale)
            blocks = [to_peer(scaled, o, 1) for o in NEAR]
            blocks[0], far_stash = barrier((blocks[0], far_stash))
    return (outputs[-1][None], grads.astype(jnp.float32)[None])


def solution(mesh):
    return jax.shard_map(
        shards,
        mesh=mesh,
        in_specs=(
            P("pipe", "tensor", None),
            P("pipe", "tensor", None),
            P("pipe", None),
            P("pipe", None),
            P("pipe", None, "tensor", None),
            P("pipe", None),
            P("pipe", "tensor", None),
            P(None, "tensor", None),
        ),
        out_specs=(P("pipe", None, "tensor", None), P("pipe", "tensor", None)),
        check_vma=False,
    )
```
